256 devices in a mesh: dp: 2 (over core), row: 16 (over x, y), col: 8 (over z).
Axes of the slice: x: 4, y: 4, z: 8, core: 2. Of those that a mesh axis runs over, the one named last changes fastest.
Arguments:
- tokens: bfloat16 [1536, 8192], P('dp', 'row'), may hold values from -6 to 6
- out_grad: bfloat16 [1536, 8192], P('dp', 'row'), may hold values from -6 to 6
- gate_weight: bfloat16 [8192, 14336], P('row', 'col'), may hold values from -0.0625 to 0.0625
- up_weight: bfloat16 [8192, 14336], P('row', 'col'), may hold values from -0.0625 to 0.0625
- down_weight: bfloat16 [14336, 8192], P('col', 'row'), may hold values from -0.046875 to 0.046875
- gate_mask: int32 [64, 112], P('row', 'col'), may hold values from 0 to 1, as said below
- up_mask: int32 [64, 112], P('row', 'col'), may hold values from 0 to 1, as said below
- down_mask: int32 [112, 64], P('col', 'row'), may hold values from 0 to 1, as said below
Outputs:
- output: bfloat16 [1536, 8192], P(('dp', 'col'), 'row')
- token_grad: bfloat16 [1536, 8192], P(('dp', 'col'), 'row')
- gate_grad: bfloat16 [8192, 14336], P('row', 'col')
- up_grad: bfloat16 [8192, 14336], P('row', 'col')
- down_grad: bfloat16 [14336, 8192], P('col', 'row')
The draws below stay inside these ranges and needn't reach their ends.
Inputs may be any that keep to these rules, and one draw needn't show every extreme that they name: `gate_mask`: one keep flag for each 128 x 128 block of the matrix; the share kept differs from block row to block row. `up_mask`: one keep flag for each 128 x 128 block of the matrix; the share kept differs from block row to block row. `down_mask`: one keep flag for each 128 x 128 block of the matrix; the share kept differs from block column to block column.
All inputs are finite; a program needn't handle non-finite values.
Results may differ from the reference program's by a relative error of at most 0.029.
Values may be sent and summed in bfloat16 or wider, within the bound.
A program may use at most 128 MiB of HBM per device.

```python
import jax
import jax.numpy as jnp
from jax import lax

D = 8192
FF = 14336
BLOCK = 128
TOK = 768
TOKENS = 1536
N_DP = 2
N_ROW = 16
N_COL = 8


def keep_flags(key, height, breadth, salt_value):
    folded = jax.random.fold_in(key, salt_value)
    first_key, second_key = jax.random.split(folded)
    keep_level = jax.random.randint(first_key, (height, 1), 1, 8)
    ballots = jax.random.randint(second_key, (height, breadth), 0, 10)
    return (ballots < keep_level).astype(jnp.int32)


def draw_gate_mask(key, part):
    return keep_flags(key, D // BLOCK, FF // BLOCK, 11)


def draw_up_mask(key, part):
    return keep_flags(key, D // BLOCK, FF // BLOCK, 12)


def draw_down_mask(key, part):
    return keep_flags(key, D // BLOCK, FF // BLOCK, 13).T


def level_of(rng, shape, cuts, least, largest):
    loudness, own = 1.0, jax.random.fold_in(rng, 6)
    for axis_at, blocks in cuts:
        heights = jnp.exp(jax.random.uniform(jax.random.fold_in(own, axis_at), (blocks,), jnp.float32, least / len(cuts), largest / len(cuts)))
        loudness = loudness * jnp.repeat(heights, shape[axis_at] // blocks).reshape([-1 if axis == axis_at else 1 for axis in range(len(shape))])
    return loudness


def bell_draw(own_key, dims, spread, bound, cuts=(), kind=jnp.bfloat16):
    loudness = level_of(own_key, dims, cuts, -0.22, 0.18) if cuts else 1.0
    values = jax.random.normal(own_key, dims, jnp.float32) * spread * loudness
    return jnp.minimum(jnp.maximum(values, -bound), bound).astype(kind)


def setup_inputs(seed: int = 0) -> dict:
    key_list = jax.random.split(jax.random.key(seed), 9)
    tokens = bell_draw(key_list[0], (TOKENS, D), 1.0, 6.0, ((0, 2), (1, 16)))
    out_grad = bell_draw(key_list[1], (TOKENS, D), 1.0, 6.0, ((0, 2), (1, 16)))
    gate_weight = bell_draw(key_list[2], (D, FF), D ** -0.5, 0.0625, ((0, 16), (1, 8)))
    up_weight = bell_draw(key_list[3], (D, FF), D ** -0.5, 0.0625, ((0, 16), (1, 8)))
    down_weight = bell_draw(key_list[4], (FF, D), FF ** -0.5, 0.046875, ((0, 8), (1, 16)))
    gate_mask = draw_gate_mask(jax.random.fold_in(key_list[8], 71), 0)
    up_mask = draw_up_mask(jax.random.fold_in(key_list[8], 71), 0)
    down_mask = draw_down_mask(jax.random.fold_in(key_list[8], 71), 0)
    return dict(tokens=tokens, out_grad=out_grad, gate_weight=gate_weight, up_weight=up_weight, down_weight=down_weight, gate_mask=gate_mask, up_mask=up_mask, down_mask=down_mask)


def expand(mask_tile):
    return jnp.repeat(jnp.repeat(mask_tile, BLOCK, axis=0), BLOCK, axis=1)


def tile_sum(pairs, parts):
    rows_out = pairs[0][0].shape[0]
    cols_out = pairs[0][1].shape[1]
    width = pairs[0][0].shape[1] // parts

    def advance(running, tile_index):
        partial_sum = jnp.zeros((rows_out, cols_out), jnp.float32)
        for left_side, right_side in pairs:
            left_piece = lax.dynamic_slice_in_dim(left_side, tile_index * width, width, 1)
            right_piece = lax.dynamic_slice_in_dim(right_side, tile_index * width, width, 0)
            partial_sum = partial_sum + jnp.dot(left_piece, right_piece, preferred_element_type=jnp.float32)
        rounded = lax.optimization_barrier(partial_sum.astype(jnp.bfloat16)).astype(jnp.float32)
        return running + rounded, None

    running, unused_out = lax.scan(advance, jnp.zeros((rows_out, cols_out), jnp.float32), jnp.arange(parts, dtype=jnp.int32))
    return running


def contract_rows(left_side, right_side):
    return lax.dot_general(left_side, right_side, (((0,), (0,)), ((), ())), preferred_element_type=jnp.float32)


def reference(tokens, out_grad, gate_weight, up_weight, down_weight, gate_mask, up_mask, down_mask):
    gate_keep = expand(gate_mask).astype(jnp.float32)
    up_keep = expand(up_mask).astype(jnp.float32)
    down_keep = expand(down_mask).astype(jnp.float32)
    gate_eff = gate_weight * gate_keep.astype(jnp.bfloat16)
    up_eff = up_weight * up_keep.astype(jnp.bfloat16)
    down_eff = down_weight * down_keep.astype(jnp.bfloat16)
    down_trans = down_eff.T
    gate_trans = gate_eff.T
    up_trans = up_eff.T
    outputs = []
    token_grads = []
    gate_total = jnp.zeros(gate_weight.shape, jnp.float32)
    up_total = jnp.zeros(up_weight.shape, jnp.float32)
    down_total = jnp.zeros(down_weight.shape, jnp.float32)
    for group in range(N_DP):
        group_in = tokens[group * TOK:(group + 1) * TOK]
        group_dy = out_grad[group * TOK:(group + 1) * TOK]
        gate_pre = tile_sum([(group_in, gate_eff)], N_ROW)
        up_pre = tile_sum([(group_in, up_eff)], N_ROW)
        gate_sig = jax.nn.sigmoid(gate_pre)
        silu_gate = gate_pre * gate_sig
        hidden = (silu_gate * up_pre).astype(jnp.bfloat16)
        outputs.append(tile_sum([(hidden, down_eff)], N_COL).astype(jnp.bfloat16))
        back = tile_sum([(group_dy, down_trans)], N_ROW)
        gate_deriv = (back * up_pre * gate_sig * (1.0 + gate_pre * (1.0 - gate_sig))).astype(jnp.bfloat16)
        up_deriv = (back * silu_gate).astype(jnp.bfloat16)
        token_grads.append(tile_sum([(gate_deriv, gate_trans), (up_deriv, up_trans)], N_COL).astype(jnp.bfloat16))
        gate_local = (contract_rows(group_in, gate_deriv) * gate_keep).astype(jnp.bfloat16)
        up_local = (contract_rows(group_in, up_deriv) * up_keep).astype(jnp.bfloat16)
        down_local = (contract_rows(hidden, group_dy) * down_keep).astype(jnp.bfloat16)
        gate_total = gate_total + gate_local.astype(jnp.float32)
        up_total = up_total + up_local.astype(jnp.float32)
        down_total = down_total + down_local.astype(jnp.float32)
    output = jnp.concatenate(outputs, axis=0)
    token_grad = jnp.concatenate(token_grads, axis=0)
    return (output, token_grad, gate_total.astype(jnp.bfloat16), up_total.astype(jnp.bfloat16), down_total.astype(jnp.bfloat16))
```

```python
import jax
import jax.numpy as jnp
from jax import lax
from jax.experimental import pallas as pl
from jax.experimental.pallas import tpu as pltpu
from jax.sharding import PartitionSpec as P

BLOCK = 128
F32 = jnp.float32
BF16 = jnp.bfloat16
MESH = pl.DeviceIdType.MESH

TOK = 768
DIM = 512
FF = 1792
HALF = FF // 2
BIG = TOK // 4
SMALL = BIG // 4
NZ = 8
ZROWS = TOK // NZ

NN = (((1,), (0,)), ((), ()))
NT = (((1,), (1,)), ((), ()))
TN = (((0,), (0,)), ((), ()))


def dot(a, b, dims=NN):
    return lax.dot_general(a, b, dims, preferred_element_type=F32)


def rows(start, size):
    return pl.ds(pl.multiple_of(start, 16), size)


def kernel(
    x_hbm, dy_hbm, gw_hbm, uw_hbm, dw_hbm, gm, um, dm,
    out_ref, dx_ref, gg_hbm, ug_hbm, dg_hbm,
    x, dy, xt, w, wd, part, q, near1, fin1, near2, fin2, share, full, d, dr, dd, ddr, o, zin, acc,
    ssem, rsem, lsem,
):
    row = lax.axis_index("row")
    zz = lax.axis_index("col")
    core = lax.axis_index("dp")
    cx, cy = row // 4, row % 4

    def rid(a, b):
        return lax.rem(a, 4) * 4 + lax.rem(b, 4)

    xm, xp = rid(cx + 3, cy), rid(cx + 1, cy)
    ym, yp = rid(cx, cy + 3), rid(cx, cy + 1)
    ring1 = ((cx, xm, xp), (cy, ym, yp))
    ring2 = ((cy, ym, yp), (cx, xm, xp))

    loads = {}

    def load(key, src, dst, i):
        cp = pltpu.make_async_copy(src, dst, lsem.at[i])
        cp.start()
        loads[key] = cp

    load("x", x_hbm, x, 0)
    load(("w", 0, 0), gw_hbm.at[:, pl.ds(0, HALF)], w.at[0, 0], 1)
    load(("w", 0, 1), gw_hbm.at[:, pl.ds(HALF, HALF)], w.at[0, 1], 2)
    load(("w", 1, 0), uw_hbm.at[:, pl.ds(0, HALF)], w.at[1, 0], 3)
    load(("w", 1, 1), uw_hbm.at[:, pl.ds(HALF, HALF)], w.at[1, 1], 4)
    load("dy", dy_hbm, dy, 5)
    load(("wd", 0), dw_hbm.at[pl.ds(0, HALF), :], wd.at[0], 6)
    load(("wd", 1), dw_hbm.at[pl.ds(HALF, HALF), :], wd.at[1], 7)

    barrier = pltpu.get_barrier_semaphore()
    for r in (xm, xp, ym, yp):
        pl.semaphore_signal(barrier, inc=1, device_id={"row": r}, device_id_type=MESH)
    pl.semaphore_signal(barrier, inc=1, device_id={"dp": 1 - core}, device_id_type=MESH)
    for k in range(1, NZ):
        pl.semaphore_signal(
            barrier, inc=1, device_id={"col": lax.rem(zz + k, NZ)}, device_id_type=MESH
        )
    pl.semaphore_wait(barrier, 4 + 1 + NZ - 1)

    sent = {}

    def send(key, src, dst, where):
        i = len(sent)
        cp = pltpu.make_async_remote_copy(
            src_ref=src, dst_ref=dst, send_sem=ssem.at[i], recv_sem=rsem.at[i],
            device_id=where, device_id_type=MESH,
        )
        cp.start()
        sent[key] = cp

    def arrived(*key):
        sent[key].wait_recv()

    def mask_cols(ref, mask, h):
        def step(j, _):
            c = pl.ds(pl.multiple_of(j * BLOCK, BLOCK), BLOCK)
            for i in range(DIM // BLOCK):
                r = pl.ds(i * BLOCK, BLOCK)
                keep = mask[i, h * 7 + j].astype(F32)
                ref[r, c] = (ref[r, c].astype(F32) * keep).astype(BF16)
            return 0

        lax.fori_loop(0, 7, step, 0)

    def mask_rows(ref, mask, h):
        def step(j, _):
            r = pl.ds(pl.multiple_of(j * BLOCK, BLOCK), BLOCK)
            for i in range(DIM // BLOCK):
                c = pl.ds(i * BLOCK, BLOCK)
                keep = mask[h * 7 + j, i].astype(F32)
                ref[r, c] = (ref[r, c].astype(F32) * keep).astype(BF16)
            return 0

        lax.fori_loop(0, 7, step, 0)

    def tiles(fn):
        def step(j, _):
            fn(pl.multiple_of(j * 256, 256), 256)
            return 0

        lax.fori_loop(0, 3, step, 0)
        fn(768, 128)

    def add_into(dst, dst_row, terms, n):
        def step(j, _):
            total = None
            for ref, at in terms:
                v = ref[rows(at + j * 48, 48), :].astype(F32)
                total = v if total is None else total + v
            dst[rows(dst_row + j * 48, 48), :] = total.astype(dst.dtype)
            return 0

        lax.fori_loop(0, n // 48, step, 0)

    def first_sends(tag, a, h, src, ring, near, fin, size, cut):
        c, m, p = ring
        far, lo, hi = lax.rem(c + 2, 4) * size, lax.rem(c + 3, 4) * size, lax.rem(c + 1, 4) * size
        rest = size - cut
        send((tag, a, h, "m1"), src.at[rows(far, cut), :], near.at[1, pl.ds(0, cut), :], {"row": m})
        send((tag, a, h, "p1"), src.at[rows(far + cut, rest), :], near.at[0, pl.ds(0, rest), :], {"row": p})
        send((tag, a, h, "m2"), src.at[rows(lo + cut, rest), :], fin.at[1, pl.ds(cut, rest), :], {"row": m})
        send((tag, a, h, "p2"), src.at[rows(hi, cut), :], fin.at[0, pl.ds(0, cut), :], {"row": p})

    def second_sends(tag, a, h, src, ring, near, fin, size, cut, adder):
        c, m, p = ring
        lo, hi = lax.rem(c + 3, 4) * size, lax.rem(c + 1, 4) * size
        rest = size - cut
        arrived(tag, a, h, "m1")
        adder(src, lo, near.at[1], cut)
        send((tag, a, h, "m3"), src.at[rows(lo, cut), :], fin.at[1, pl.ds(0, cut), :], {"row": m})
        arrived(tag, a, h, "p1")
        adder(src, hi + cut, near.at[0], rest)
        send((tag, a, h, "p3"), src.at[rows(hi + cut, rest), :], fin.at[0, pl.ds(cut, rest), :], {"row": p})

    def last_arrivals(tag, a, h):
        for k in ("m2", "p2", "m3", "p3"):
            arrived(tag, a, h, k)

    def add_big(src, at, near, n):
        add_into(src, at, ((src, at), (near, 0)), n)

    def add_small(src, at, near, n):
        src[rows(at, n), :] = (
            src[rows(at, n), :].astype(F32) + near[pl.ds(0, n), :].astype(F32)
        ).astype(BF16)

    def cut2(a, h):
        return 32 if (a + h) % 2 == 0 else 16

    def s0(a, h):
        dst = part.at[a, h]
        if a < 2:
            loads[("w", a, h)].wait()
            mask_cols(w.at[a, h], (gm, um)[a], h)

            def tile(n, size):
                c = pl.ds(n, size)
                dst[:, c] = dot(x[...], w[a, h, :, c]).astype(BF16)
        else:
            loads[("wd", h)].wait()
            mask_rows(wd.at[h], dm, h)

            def tile(n, size):
                c = pl.ds(n, size)
                dst[:, c] = dot(dy[...], wd[h, c, :], NT).astype(BF16)

        tiles(tile)
        first_sends("r1", a, h, dst, ring1[h], near1.at[a, h], fin1.at[a, h], BIG, BIG // 2)

    def s1(a, h):
        second_sends(
            "r1", a, h, part.at[a, h], ring1[h], near1.at[a, h], fin1.at[a, h], BIG, BIG // 2, add_big
        )

    def s2(a, h):
        last_arrivals("r1", a, h)
        add_into(
            q.at[a, h], 0,
            ((part.at[a, h], ring1[h][0] * BIG), (fin1.at[a, h, 0], 0), (fin1.at[a, h, 1], 0)), BIG,
        )
        first_sends("r2", a, h, q.at[a, h], ring2[h], near2.at[a, h], fin2.at[a, h], SMALL, cut2(a, h))

    def s3(a, h):
        second_sends(
            "r2", a, h, q.at[a, h], ring2[h], near2.at[a, h], fin2.at[a, h], SMALL, cut2(a, h), add_small
        )

    def s4(a, h):
        last_arrivals("r2", a, h)
        share[a, h] = (
            q[a, h, rows(ring2[h][0] * SMALL, SMALL), :].astype(F32)
            + fin2[a, h, 0].astype(F32)
            + fin2[a, h, 1].astype(F32)
        )

    def own(h):
        return ring1[h][0] * BIG + ring2[h][0] * SMALL

    def gather_sends(tag, g, h, ring, base, size):
        c, m, p = ring
        here = full.at[g, h, rows(base + c * size, size), :]
        send((tag, g, h, "m1"), here, here, {"row": m})
        send((tag, g, h, "p1"), here, here, {"row": p})

    def gather_passes(tag, g, h, ring, base, size, cut):
        c, m, p = ring
        lo, hi = lax.rem(c + 3, 4) * size, lax.rem(c + 1, 4) * size
        arrived(tag, g, h, "p1")
        there = full.at[g, h, rows(base + lo, cut), :]
        send((tag, g, h, "p2"), there, there, {"row": p})
        arrived(tag, g, h, "m1")
        there = full.at[g, h, rows(base + hi + cut, size - cut), :]
        send((tag, g, h, "m2"), there, there, {"row": m})

    def s5(g, h):
        gather_sends("g2", g, h, ring2[h], ring1[h][0] * BIG, SMALL)

    def s6(g, h):
        gather_passes("g2", g, h, ring2[h], ring1[h][0] * BIG, SMALL, cut2(g, h))

    def s7(g, h):
        arrived("g2", g, h, "p2")
        arrived("g2", g, h, "m2")
        gather_sends("g1", g, h, ring1[h], 0, BIG)

    def s8(g, h):
        gather_passes("g1", g, h, ring1[h], 0, BIG, BIG // 2)

    def s9(g, h):
        arrived("g1", g, h, "p2")
        arrived("g1", g, h, "m2")

    def make_hidden(h):
        gate, up = share[0, h], share[1, h]
        full[0, h, rows(own(h), SMALL), :] = (gate * jax.nn.sigmoid(gate) * up).astype(BF16)

    def make_grads(h):
        gate, up, back = share[0, h], share[1, h], share[2, h]
        sig = jax.nn.sigmoid(gate)
        full[1, h, rows(own(h), SMALL), :] = (
            back * up * sig * (1.0 + gate * (1.0 - sig))
        ).astype(BF16)
        full[2, h, rows(own(h), SMALL), :] = (back * (gate * sig)).astype(BF16)

    def scatter_z(k):
        for s in range(1, NZ):
            peer = lax.rem(zz + s, NZ)
            send(("z", k, s), o.at[k, rows(peer * ZROWS, ZROWS), :], zin.at[k, s - 1], {"col": peer})

    def finish_z(k, ref):
        for s in range(1, NZ):
            arrived("z", k, s)
        total = o[k, rows(zz * ZROWS, ZROWS), :].astype(F32)
        for s in range(1, NZ):
            total = total + zin[k, s - 1].astype(F32)
        ref[...] = total.astype(BF16)

    def out_part():
        def step(j, _):
            r = rows(j * 384, 384)
            o[0, r, :] = (dot(full[0, 0, r, :], wd[0]) + dot(full[0, 1, r, :], wd[1])).astype(BF16)
            return 0

        lax.fori_loop(0, 2, step, 0)
        scatter_z(0)

    def dx_part(g):
        def step(j, _):
            r = rows(j * 384, 384)
            v = dot(full[g, 0, r, :], w[g - 1, 0], NT) + dot(full[g, 1, r, :], w[g - 1, 1], NT)
            if g == 1:
                acc[r, :] = v
            else:
                o[1, r, :] = (acc[r, :] + v).astype(BF16)
            return 0

        lax.fori_loop(0, 2, step, 0)
        if g == 2:
            scatter_z(1)

    def grad_down(h):
        def tile(n, size):
            v = dot(full[0, h, :, pl.ds(n, size)], dy[...], TN)
            for jj in range(size // BLOCK):
                for i in range(DIM // BLOCK):
                    keep = dm[h * 7 + n // BLOCK + jj, i].astype(F32)
                    c = pl.ds(i * BLOCK, BLOCK)
                    dd[h, pl.ds(n + jj * BLOCK, BLOCK), c] = (
                        v[jj * BLOCK : (jj + 1) * BLOCK, i * BLOCK : (i + 1) * BLOCK] * keep
                    ).astype(BF16)

        tiles(tile)
        send(("d", 2, h), dd.at[h], ddr.at[h], {"dp": 1 - core})

    def grad_cols(a, h):
        mask = (gm, um)[a]

        def tile(n, size):
            v = dot(xt[...], full[a + 1, h, :, pl.ds(n, size)])
            for jj in range(size // BLOCK):
                for i in range(DIM // BLOCK):
                    keep = mask[i, h * 7 + n // BLOCK + jj].astype(F32)
                    r = pl.ds(i * BLOCK, BLOCK)
                    d[a, h, r, pl.ds(n + jj * BLOCK, BLOCK)] = (
                        v[i * BLOCK : (i + 1) * BLOCK, jj * BLOCK : (jj + 1) * BLOCK] * keep
                    ).astype(BF16)

        tiles(tile)
        send(("d", a, h), d.at[a, h], dr.at[a, h], {"dp": 1 - core})

    stores = []

    def finish_grad(a, h):
        arrived("d", a, h)
        sent[("d", a, h)].wait_send()
        mine, other = (d.at[a, h], dr.at[a, h]) if a < 2 else (dd.at[h], ddr.at[h])
        n = DIM if a < 2 else HALF

        def step(j, _):
            r = rows(j * 64, 64)
            mine[r, :] = (mine[r, :].astype(F32) + other[r, :].astype(F32)).astype(BF16)
            return 0

        lax.fori_loop(0, n // 64, step, 0)
        if a < 2:
            target = (gg_hbm, ug_hbm)[a].at[:, pl.ds(h * HALF, HALF)]
        else:
            target = dg_hbm.at[pl.ds(h * HALF, HALF), :]
        cp = pltpu.make_async_copy(mine, target, lsem.at[8 + a * 2 + h])
        cp.start()
        stores.append(cp)

    def both(fn, *args):
        fn(*args, 0)
        fn(*args, 1)

    loads["x"].wait()
    both(s0, 0)
    both(s0, 1)
    both(s1, 0)
    loads["dy"].wait()
    both(s0, 2)
    both(s1, 1)
    both(s2, 0)
    both(s1, 2)
    both(s3, 0)
    both(s2, 1)
    both(s4, 0)
    both(s3, 1)
    both(s2, 2)
    both(s4, 1)
    both(make_hidden)
    both(s5, 0)
    both(s3, 2)
    both(s6, 0)
    both(s4, 2)
    both(make_grads)
    both(s5, 1)
    both(s7, 0)
    both(s5, 2)
    both(s6, 1)
    both(s6, 2)
    for i in range(DIM // BLOCK):
        xt[pl.ds(i * BLOCK, BLOCK), :] = x[:, pl.ds(i * BLOCK, BLOCK)].T
    both(s7, 1)
    both(s8, 0)
    both(s7, 2)
    both(s9, 0)
    out_part()
    both(s8, 1)
    both(grad_down)
    both(s8, 2)
    both(s9, 1)
    dx_part(1)
    both(grad_cols, 0)
    both(finish_grad, 2)
    both(s9, 2)
    dx_part(2)
    both(grad_cols, 1)
    both(finish_grad, 0)
    finish_z(0, out_ref)
    both(finish_grad, 1)
    finish_z(1, dx_ref)
    for key, cp in sent.items():
        if key[0] != "d":
            cp.wait_send()
    for cp in stores:
        cp.wait()


N_SENDS = 3 * 2 * 2 * 6 + 3 * 2 * 2 * 4 + 2 * (NZ - 1) + 6


def body(tokens, out_grad, gate_weight, up_weight, down_weight, gate_mask, up_mask, down_mask):
    hbm = pl.BlockSpec(memory_space=pl.ANY)
    smem = pl.BlockSpec(memory_space=pltpu.SMEM)
    vmem = pl.BlockSpec(memory_space=pltpu.VMEM)
    return pl.pallas_call(
        kernel,
        out_shape=(
            jax.ShapeDtypeStruct((ZROWS, DIM), BF16),
            jax.ShapeDtypeStruct((ZROWS, DIM), BF16),
            jax.ShapeDtypeStruct((DIM, FF), BF16),
            jax.ShapeDtypeStruct((DIM, FF), BF16),
            jax.ShapeDtypeStruct((FF, DIM), BF16),
        ),
        in_specs=[hbm] * 5 + [smem] * 3,
        out_specs=(vmem, vmem, hbm, hbm, hbm),
        scratch_shapes=[
            pltpu.VMEM((TOK, DIM), BF16),
            pltpu.VMEM((TOK, DIM), BF16),
            pltpu.VMEM((DIM, TOK), BF16),
            pltpu.VMEM((2, 2, DIM, HALF), BF16),
            pltpu.VMEM((2, HALF, DIM), BF16),
            pltpu.VMEM((3, 2, TOK, HALF), BF16),
            pltpu.VMEM((3, 2, BIG, HALF), BF16),
            pltpu.VMEM((3, 2, 2, BIG // 2, HALF), BF16),
            pltpu.VMEM((3, 2, 2, BIG, HALF), BF16),
            pltpu.VMEM((3, 2, 2, 32, HALF), BF16),
            pltpu.VMEM((3, 2, 2, SMALL, HALF), BF16),
            pltpu.VMEM((3, 2, SMALL, HALF), F32),
            pltpu.VMEM((3, 2, TOK, HALF), BF16),
            pltpu.VMEM((2, 2, DIM, HALF), BF16),
            pltpu.VMEM((2, 2, DIM, HALF), BF16),
            pltpu.VMEM((2, HALF, DIM), BF16),
            pltpu.VMEM((2, HALF, DIM), BF16),
            pltpu.VMEM((2, TOK, DIM), BF16),
            pltpu.VMEM((2, NZ - 1, ZROWS, DIM), BF16),
            pltpu.VMEM((TOK, DIM), F32),
            pltpu.SemaphoreType.DMA((N_SENDS,)),
            pltpu.SemaphoreType.DMA((N_SENDS,)),
            pltpu.SemaphoreType.DMA((14,)),
        ],
        compiler_params=pltpu.CompilerParams(
            collective_id=0, has_side_effects=True, vmem_limit_bytes=66_000_000
        ),
    )(tokens, out_grad, gate_weight, up_weight, down_weight, gate_mask, up_mask, down_mask)


def solution(mesh):
    placed = (
        P("dp", "row"),
        P("dp", "row"),
        P("row", "col"),
        P("row", "col"),
        P("col", "row"),
        P("row", "col"),
        P("row", "col"),
        P("col", "row"),
    )
    return jax.shard_map(
        body,
        mesh=mesh,
        in_specs=placed,
        out_specs=(
            P(("dp", "col"), "row"),
            P(("dp", "col"), "row"),
            P("row", "col"),
            P("row", "col"),
            P("col", "row"),
        ),
        check_vma=False,
    )
```

```python
import jax
import jax.numpy as jnp
from jax import lax
from jax.experimental import pallas as pl
from jax.experimental.pallas import tpu as pltpu
from jax.sharding import PartitionSpec as P

BLOCK = 128
VMEM_LIMIT = 49000000
F32 = jnp.float32
BF16 = jnp.bfloat16
MESH = pl.DeviceIdType.MESH

TOK = 768
DIM = 512
FF = 1792
HALF = FF // 2
BIG = TOK // 4
SMALL = BIG // 4
NZ = 8
ZROWS = TOK // NZ

NN = (((1,), (0,)), ((), ()))
NT = (((1,), (1,)), ((), ()))
TN = (((0,), (0,)), ((), ()))


def dot(a, b, dims=NN):
    return lax.dot_general(a, b, dims, preferred_element_type=F32)


def rows(start, size):
    return pl.ds(pl.multiple_of(start, 16), size)


def kernel(
    x_hbm, dy_hbm, gw_hbm, uw_hbm, dw_hbm, gm, um, dm,
    out_ref, dx_ref, gg, ug, dg,
    x, dy, xt, w, wd, part, q, near1, fin1, near2, fin2, share, full, dr, ddr, o, zin, odx, zdx, acc,
    ssem, rsem, lsem,
):
    row = lax.axis_index("row")
    zz = lax.axis_index("col")
    core = lax.axis_index("dp")
    cx, cy = row // 4, row % 4

    def rid(a, b):
        return lax.rem(a, 4) * 4 + lax.rem(b, 4)

    xm, xp = rid(cx + 3, cy), rid(cx + 1, cy)
    ym, yp = rid(cx, cy + 3), rid(cx, cy + 1)
    ring1 = ((cx, xm, xp), (cy, ym, yp))
    ring2 = ((cy, ym, yp), (cx, xm, xp))

    loads = {}
    loaded = set()

    def load(key, src, dst, i):
        cp = pltpu.make_async_copy(src, dst, lsem.at[i])
        cp.start()
        loads[key] = cp

    load("x", x_hbm, x, 0)
    load(("w", 0, 0), gw_hbm.at[:, pl.ds(0, HALF)], w.at[0, 0], 1)
    load(("w", 0, 1), gw_hbm.at[:, pl.ds(HALF, HALF)], w.at[0, 1], 2)
    load(("w", 1, 0), uw_hbm.at[:, pl.ds(0, HALF)], w.at[1, 0], 3)
    load(("w", 1, 1), uw_hbm.at[:, pl.ds(HALF, HALF)], w.at[1, 1], 4)
    load("dy", dy_hbm, dy, 5)
    load(("wd", 0), dw_hbm.at[pl.ds(0, HALF), :], wd.at[0], 6)
    load(("wd", 1), dw_hbm.at[pl.ds(HALF, HALF), :], wd.at[1], 7)

    barrier = pltpu.get_barrier_semaphore()
    for r in (xm, xp, ym, yp):
        pl.semaphore_signal(barrier, inc=1, device_id={"row": r}, device_id_type=MESH)
    pl.semaphore_signal(barrier, inc=1, device_id={"dp": 1 - core}, device_id_type=MESH)
    for k in range(1, NZ):
        pl.semaphore_signal(
            barrier, inc=1, device_id={"col": lax.rem(zz + k, NZ)}, device_id_type=MESH
        )
    pl.semaphore_wait(barrier, 4 + 1 + NZ - 1)

    sent = {}

    def send(key, src, dst, where):
        i = len(sent)
        cp = pltpu.make_async_remote_copy(
            src_ref=src, dst_ref=dst, send_sem=ssem.at[i], recv_sem=rsem.at[i],
            device_id=where, device_id_type=MESH,
        )
        cp.start()
        sent[key] = cp

    got = set()

    def arrived(*key):
        got.add(key)
        sent[key].wait_recv()

    def splat(flag):
        return jnp.full((BLOCK, BLOCK), flag.astype(F32), F32).astype(BF16)

    def mask_cols(ref, mask, h):
        def step(j, _):
            c = pl.ds(pl.multiple_of(j * BLOCK, BLOCK), BLOCK)
            for i in range(DIM // BLOCK):
                r = pl.ds(i * BLOCK, BLOCK)
                ref[r, c] = ref[r, c] * splat(mask[i, h * 7 + j])
            return 0

        lax.fori_loop(0, 7, step, 0)

    def mask_rows(ref, mask, h):
        def step(j, _):
            r = pl.ds(pl.multiple_of(j * BLOCK, BLOCK), BLOCK)
            for i in range(DIM // BLOCK):
                c = pl.ds(i * BLOCK, BLOCK)
                ref[r, c] = ref[r, c] * splat(mask[i, h * 7 + j])
            return 0

        lax.fori_loop(0, 7, step, 0)

    def tiles(fn):
        def step(j, _):
            fn(pl.multiple_of(j * 256, 256), 256)
            return 0

        lax.fori_loop(0, 3, step, 0)
        fn(768, 128)

    def add_into(dst, dst_row, terms, n):
        def step(j, _):
            total = None
            for ref, at in terms:
                v = ref[rows(at + j * 48, 48), :].astype(F32)
                total = v if total is None else total + v
            dst[rows(dst_row + j * 48, 48), :] = total.astype(dst.dtype)
            return 0

        lax.fori_loop(0, n // 48, step, 0)

    def near_sends(tag, a, h, src, ring, near, fin, size, cut):
        c, m, p = ring
        far, rest = lax.rem(c + 2, 4) * size, size - cut
        send((tag, a, h, "m1"), src.at[rows(far, cut), :], near.at[1, pl.ds(0, cut), :], {"row": m})
        send((tag, a, h, "p1"), src.at[rows(far + cut, rest), :], near.at[0, pl.ds(0, rest), :], {"row": p})

    def next_sends(tag, a, h, src, ring, near, fin, size, cut):
        c, m, p = ring
        lo, hi, rest = lax.rem(c + 3, 4) * size, lax.rem(c + 1, 4) * size, size - cut
        send((tag, a, h, "m2"), src.at[rows(lo + cut, rest), :], fin.at[1, pl.ds(cut, rest), :], {"row": m})
        send((tag, a, h, "p2"), src.at[rows(hi, cut), :], fin.at[0, pl.ds(0, cut), :], {"row": p})

    def second_sends(tag, a, h, src, ring, near, fin, size, cut, adder):
        c, m, p = ring
        lo, hi = lax.rem(c + 3, 4) * size, lax.rem(c + 1, 4) * size
        rest = size - cut
        arrived(tag, a, h, "m1")
        adder(src, lo, near.at[1], cut)
        send((tag, a, h, "m3"), src.at[rows(lo, cut), :], fin.at[1, pl.ds(0, cut), :], {"row": m})
        arrived(tag, a, h, "p1")
        adder(src, hi + cut, near.at[0], rest)
        send((tag, a, h, "p3"), src.at[rows(hi + cut, rest), :], fin.at[0, pl.ds(cut, rest), :], {"row": p})

    def last_arrivals(tag, a, h):
        for k in ("m2", "p2", "m3", "p3"):
            arrived(tag, a, h, k)

    def add_big(src, at, near, n):
        add_into(src, at, ((src, at), (near, 0)), n)

    def add_small(src, at, near, n):
        src[rows(at, n), :] = (
            src[rows(at, n), :].astype(F32) + near[pl.ds(0, n), :].astype(F32)
        ).astype(BF16)

    def cut2(a, h):
        return 32 if (a + h) % 2 == 0 else 16

    def first_args(a, h):
        return "r1", a, h, part.at[a, h], ring1[h], near1.at[a, h], fin1.at[a, h], BIG, BIG // 2

    def compute(a, h):
        dst = part.at[a, h]
        if a < 2:
            wait_load(("w", a, h))
            mask_cols(w.at[a, h], (gm, um)[a], h)

            def tile(n, size):
                c = pl.ds(n, size)
                dst[:, c] = dot(x[...], w[a, h, :, c]).astype(BF16)
        else:
            wait_load(("wd", h))
            mask_rows(wd.at[h], dm, h)

            def tile(n, size):
                c = pl.ds(n, size)
                dst[:, c] = dot(dy[...], wd[h, c, :], NT).astype(BF16)

        tiles(tile)

    def start_sends(a, h):
        near_sends(*first_args(a, h))
        next_sends(*first_args(a, h))

    def start_gate():
        def chunk(h, k):
            r = rows(lax.rem(ring1[h][0] + k, 4) * BIG, BIG)
            part[0, h, r, :] = dot(x[r, :], w[0, h]).astype(BF16)

        for h in range(2):
            wait_load(("w", 0, h))
            mask_cols(w.at[0, h], gm, h)
            chunk(h, 2)
            near_sends(*first_args(0, h))
        for h in range(2):
            chunk(h, 3)
            chunk(h, 1)
            next_sends(*first_args(0, h))
        for h in range(2):
            chunk(h, 0)

    def s1(a, h):
        second_sends(
            "r1", a, h, part.at[a, h], ring1[h], near1.at[a, h], fin1.at[a, h], BIG, BIG // 2, add_big
        )

    def s2(a, h):
        last_arrivals("r1", a, h)
        add_into(
            q.at[a, h], 0,
            ((part.at[a, h], ring1[h][0] * BIG), (fin1.at[a, h, 0], 0), (fin1.at[a, h, 1], 0)), BIG,
        )
        args = "r2", a, h, q.at[a, h], ring2[h], near2.at[a, h], fin2.at[a, h], SMALL, cut2(a, h)
        near_sends(*args)
        next_sends(*args)

    def s3(a, h):
        second_sends(
            "r2", a, h, q.at[a, h], ring2[h], near2.at[a, h], fin2.at[a, h], SMALL, cut2(a, h), add_small
        )

    def s4(a, h):
        last_arrivals("r2", a, h)
        share[a, h] = (
            q[a, h, rows(ring2[h][0] * SMALL, SMALL), :].astype(F32)
            + fin2[a, h, 0].astype(F32)
            + fin2[a, h, 1].astype(F32)
        )

    def block(g, h, k, b):
        return full.at[g, h, k, b // 2, lax.rem(b, 2)]

    def s5(g, h):
        c, m, p = ring2[h]
        here = block(g, h, ring1[h][0], c)
        send(("g2", g, h, "m1"), here, here, {"row": m})
        send(("g2", g, h, "p1"), here, here, {"row": p})

    def s6(g, h):
        c, m, p = ring2[h]
        k, cut = ring1[h][0], cut2(g, h)
        arrived("g2", g, h, "p1")
        there = block(g, h, k, lax.rem(c + 3, 4)).at[pl.ds(0, cut), :]
        send(("g2", g, h, "p2"), there, there, {"row": p})
        arrived("g2", g, h, "m1")
        there = block(g, h, k, lax.rem(c + 1, 4)).at[pl.ds(cut, SMALL - cut), :]
        send(("g2", g, h, "m2"), there, there, {"row": m})

    def s7(g, e, h):
        if e == 0:
            arrived("g2", g, h, "p2")
            arrived("g2", g, h, "m2")
        c, m, p = ring1[h]
        here = full.at[g, h, c, :, e]
        send(("g1", g, e, h, "m1"), here, here, {"row": m})
        send(("g1", g, e, h, "p1"), here, here, {"row": p})

    def s8(g, e, h):
        c, m, p = ring1[h]
        arrived("g1", g, e, h, "p1")
        there = full.at[g, h, lax.rem(c + 3, 4), 0, e]
        send(("g1", g, e, h, "p2"), there, there, {"row": p})
        arrived("g1", g, e, h, "m1")
        there = full.at[g, h, lax.rem(c + 1, 4), 1, e]
        send(("g1", g, e, h, "m2"), there, there, {"row": m})

    def s9(g, e, h):
        arrived("g1", g, e, h, "p2")
        arrived("g1", g, e, h, "m2")

    def own(g, h):
        return block(g, h, ring1[h][0], ring2[h][0])

    def make_hidden(h):
        gate, up = share[0, h], share[1, h]
        own(0, h)[...] = (gate * jax.nn.sigmoid(gate) * up).astype(BF16)

    def make_grads(h):
        gate, up, back = share[0, h], share[1, h], share[2, h]
        sig = jax.nn.sigmoid(gate)
        own(1, h)[...] = (back * up * sig * (1.0 + gate * (1.0 - sig))).astype(BF16)
        own(2, h)[...] = (back * (gate * sig)).astype(BF16)

    def z_out():
        for i in range(1, NZ):
            peer = lax.rem(zz + i, NZ)
            send(("z", i), o.at[rows(peer * ZROWS, ZROWS), :], zin.at[i - 1], {"col": peer})

    def z_dx(e):
        for i in range(1, NZ):
            peer = lax.rem(zz + i, NZ)
            send(("z", e, i), odx.at[e, peer], zdx.at[e, i - 1], {"col": peer})

    def finish_out():
        for i in range(1, NZ):
            arrived("z", i)
        total = o[rows(zz * ZROWS, ZROWS), :].astype(F32)
        for i in range(1, NZ):
            total = total + zin[i - 1].astype(F32)
        out_ref[...] = total.astype(BF16)

    def finish_dx(e):
        for i in range(1, NZ):
            arrived("z", e, i)
        total = odx[e, zz].astype(F32)
        for i in range(1, NZ):
            total = total + zdx[e, i - 1].astype(F32)
        dx_ref[pl.ds(e * 48, 48), :] = total.astype(BF16)

    def out_part():
        def step(j, _):
            k = pl.ds(2 * j, 2)
            o[rows(j * 384, 384), :] = (
                dot(full[0, 0, k].reshape(384, HALF), wd[0])
                + dot(full[0, 1, k].reshape(384, HALF), wd[1])
            ).astype(BF16)
            return 0

        lax.fori_loop(0, 2, step, 0)
        z_out()

    def dx_part(g, e):
        def term(h):
            return dot(full[g, h, :, :, e].reshape(384, HALF), w[g - 1, h], NT)

        v = term(0) + term(1)
        if g == 1:
            acc[...] = v
        else:
            odx[e] = (acc[...] + v).astype(BF16).reshape(NZ, 48, DIM)
            z_dx(e)

    def mine(a, h):
        part_of = pl.ds(h * HALF, HALF)
        return (gg, ug)[a].at[:, part_of] if a < 2 else dg.at[part_of, :]

    def grad_down(h):
        def tile(n, size):
            v = dot(full[0, h, :, :, :, :, pl.ds(n, size)].reshape(TOK, size), dy[...], TN)
            for jj in range(size // BLOCK):
                for i in range(DIM // BLOCK):
                    keep = dm[i, h * 7 + n // BLOCK + jj].astype(F32)
                    c = pl.ds(i * BLOCK, BLOCK)
                    dg[pl.ds(h * HALF + n + jj * BLOCK, BLOCK), c] = (
                        v[jj * BLOCK : (jj + 1) * BLOCK, i * BLOCK : (i + 1) * BLOCK] * keep
                    ).astype(BF16)

        tiles(tile)
        send(("d", 2, h), mine(2, h), ddr.at[h], {"dp": 1 - core})

    def grad_cols(a, h):
        mask = (gm, um)[a]

        def tile(n, size):
            v = dot(xt[...], full[a + 1, h, :, :, :, :, pl.ds(n, size)].reshape(TOK, size))
            for jj in range(size // BLOCK):
                for i in range(DIM // BLOCK):
                    keep = mask[i, h * 7 + n // BLOCK + jj].astype(F32)
                    r = pl.ds(i * BLOCK, BLOCK)
                    (gg, ug)[a][r, pl.ds(h * HALF + n + jj * BLOCK, BLOCK)] = (
                        v[i * BLOCK : (i + 1) * BLOCK, jj * BLOCK : (jj + 1) * BLOCK] * keep
                    ).astype(BF16)

        tiles(tile)
        send(("d", a, h), mine(a, h), dr.at[a, h], {"dp": 1 - core})

    def finish_grad(a, h):
        arrived("d", a, h)
        sent[("d", a, h)].wait_send()
        here, other = mine(a, h), (dr.at[a, h] if a < 2 else ddr.at[h])
        n = DIM if a < 2 else HALF

        def step(j, _):
            r = rows(j * 64, 64)
            here[r, :] = (here[r, :].astype(F32) + other[r, :].astype(F32)).astype(BF16)
            return 0

        lax.fori_loop(0, n // 64, step, 0)

    def both(fn, *args):
        fn(*args, 0)
        fn(*args, 1)

    def wait_load(name):
        loaded.add(name)
        loads[name].wait()

    def transpose_x():
        for i in range(DIM // BLOCK):
            xt[pl.ds(i * BLOCK, BLOCK), :] = x[:, pl.ds(i * BLOCK, BLOCK)].T

    def one(fn, *args):
        return (fn, *args)

    def two(fn, *args):
        return (both, fn, *args)

    steps = [
        one(wait_load, "x"),
        one(start_gate),
        two(compute, 1), two(start_sends, 1),
        two(s1, 0),
        one(wait_load, "dy"),
        two(compute, 2),
        two(s1, 1), two(s2, 0), two(start_sends, 2), two(s3, 0), two(s2, 1), two(s4, 0),
        two(s3, 1), two(s4, 1),
        two(make_hidden), two(s5, 0),
        two(s1, 2), two(s6, 0), two(s7, 0, 0), two(s2, 2), two(s7, 0, 1), two(s3, 2), two(s8, 0, 0),
        two(s4, 2),
        two(make_grads), two(s5, 1), two(s5, 2), two(s8, 0, 1), two(s6, 1), two(s6, 2),
        two(s7, 1, 0), two(s7, 2, 0),
        two(s9, 0, 0), two(s9, 0, 1),
        one(out_part),
        two(s8, 1, 0), two(s7, 1, 1),
        one(transpose_x),
        two(s8, 2, 0), two(s7, 2, 1),
        one(grad_down, 0),
        two(s9, 1, 0),
        one(dx_part, 1, 0),
        two(s8, 1, 1),
        two(s9, 2, 0),
        one(dx_part, 2, 0),
        two(s8, 2, 1),
        one(grad_down, 1),
        two(s9, 1, 1),
        one(dx_part, 1, 1),
        two(s9, 2, 1),
        one(dx_part, 2, 1),
        two(grad_cols, 0),
        one(finish_out),
        two(finish_grad, 2),
        two(grad_cols, 1),
        two(finish_grad, 0),
        one(finish_dx, 0),
        two(finish_grad, 1),
        one(finish_dx, 1),
    ]
    for fn, *args in steps:
        fn(*args)
    for key, cp in sent.items():
        if key not in got:
            cp.wait_recv()
        if key[0] != "d" or key not in got:
            cp.wait_send()
    for key in loads:
        if key not in loaded:
            loads[key].wait()


N_SENDS = 3 * 2 * 2 * 6 + 3 * 2 * 3 * 4 + 3 * (NZ - 1) + 6


def move(*refs):
    copies = [pltpu.make_async_copy(refs[k], refs[5 + k], refs[10].at[k]) for k in range(5)]
    for cp in copies:
        cp.start()
    for cp in copies:
        cp.wait()


def body(tokens, out_grad, gate_weight, up_weight, down_weight, gate_mask, up_mask, down_mask):
    hbm = pl.BlockSpec(memory_space=pltpu.HBM)
    smem = pl.BlockSpec(memory_space=pltpu.SMEM)
    vmem = pl.BlockSpec(memory_space=pltpu.VMEM)
    shapes = ((ZROWS, DIM), (ZROWS, DIM), (DIM, FF), (DIM, FF), (FF, DIM))
    results = tuple(jax.ShapeDtypeStruct(shape, BF16) for shape in shapes)
    made = pl.pallas_call(
        kernel,
        out_shape=results,
        in_specs=[hbm] * 5 + [smem] * 3,
        out_specs=(vmem,) * 5,
        scratch_shapes=[
            pltpu.VMEM((TOK, DIM), BF16),
            pltpu.VMEM((TOK, DIM), BF16),
            pltpu.VMEM((DIM, TOK), BF16),
            pltpu.VMEM((2, 2, DIM, HALF), BF16),
            pltpu.VMEM((2, HALF, DIM), BF16),
            pltpu.VMEM((3, 2, TOK, HALF), BF16),
            pltpu.VMEM((3, 2, BIG, HALF), BF16),
            pltpu.VMEM((3, 2, 2, BIG // 2, HALF), BF16),
            pltpu.VMEM((3, 2, 2, BIG, HALF), BF16),
            pltpu.VMEM((3, 2, 2, 32, HALF), BF16),
            pltpu.VMEM((3, 2, 2, SMALL, HALF), BF16),
            pltpu.VMEM((3, 2, SMALL, HALF), F32),
            pltpu.VMEM((3, 2, 4, 2, 2, SMALL, HALF), BF16),
            pltpu.VMEM((2, 2, DIM, HALF), BF16),
            pltpu.VMEM((2, HALF, DIM), BF16),
            pltpu.VMEM((TOK, DIM), BF16),
            pltpu.VMEM((NZ - 1, ZROWS, DIM), BF16),
            pltpu.VMEM((2, NZ, 48, DIM), BF16),
            pltpu.VMEM((2, NZ - 1, 48, DIM), BF16),
            pltpu.VMEM((TOK // 2, DIM), F32),
            pltpu.SemaphoreType.DMA((N_SENDS,)),
            pltpu.SemaphoreType.DMA((N_SENDS,)),
            pltpu.SemaphoreType.DMA((8,)),
        ],
        compiler_params=pltpu.CompilerParams(
            collective_id=0, has_side_effects=True, vmem_limit_bytes=VMEM_LIMIT
        ),
    )(tokens, out_grad, gate_weight, up_weight, down_weight, gate_mask, up_mask, down_mask.T)
    return pl.pallas_call(
        move,
        out_shape=results,
        in_specs=[vmem] * 5,
        out_specs=[hbm] * 5,
        scratch_shapes=[pltpu.SemaphoreType.DMA((5,))],
        compiler_params=pltpu.CompilerParams(vmem_limit_bytes=1 << 20),
    )(*made)


def solution(mesh):
    placed = (
        P("dp", "row"),
        P("dp", "row"),
        P("row", "col"),
        P("row", "col"),
        P("col", "row"),
        P("row", "col"),
        P("row", "col"),
        P("col", "row"),
    )
    return jax.shard_map(
        body,
        mesh=mesh,
        in_specs=placed,
        out_specs=(
            P(("dp", "col"), "row"),
            P(("dp", "col"), "row"),
            P("row", "col"),
            P("row", "col"),
            P("col", "row"),
        ),
        check_vma=False,
    )
```
